128 devices in a mesh: dp: 128 (over z, y, x, core).
Axes of the slice: x: 4, y: 4, z: 4, core: 2. Of those that a mesh axis runs over, the one named last changes fastest.
Arguments:
- gradient: float32 [128, 16384, 128], P('dp'), may hold values from -6 to 6
- residual: float32 [128, 16384, 128], P('dp'), may hold values from -5 to 5
- weights: float32 [16384, 128], replicated, may hold values from -6 to 6
- momentum: float32 [16384, 128], replicated, may hold values from -6 to 6
- sel_idx: int32 [128, 128, 4], replicated, may hold values from 0 to 16383, as said below
- sel_count: int32 [128, 128], replicated, may hold values from 1 to 4, as said below
- gath_idx: int32 [128, 8], replicated, may hold values from 0 to 16383, as said below
- gath_count: int32 [128], replicated, may hold values from 6 to 8, as said below
Outputs:
- new_weights: float32 [16384, 128], replicated
- new_momentum: float32 [16384, 128], replicated
- new_residual: float32 [128, 16384, 128], P('dp')
The draws below stay inside these ranges and needn't reach their ends.
Inputs may be any that keep to these rules, and one draw needn't show every extreme that they name: Owners' regions are consecutive runs of blocks in owner order covering all 16384 blocks, each of 64 to 192 blocks, some of exactly 192. All 4 entries of sel_idx[s, o] are distinct entries of gath_idx[o], those at or beyond sel_count[s, o] included. `sel_count`: some owner receives exactly 4 used slots from every replica. All 8 entries of gath_idx[o] are distinct blocks of owner o's region. `gath_count`: some owner lists exactly 8 blocks.
All inputs are finite; a program needn't handle non-finite values.
Results may differ from the reference program's by a relative error of at most 0.00002.
Values sent between devices are 32-bit elements; how exact they have to be, the bound alone decides.
No kernel may reach another device: no remote copies, remote signals or barrier semaphores. Data moves between devices by JAX's collectives and lax.ppermute only.
A program may use at most 192 MiB of HBM per device.

```python
import jax
import jax.numpy as jnp
from jax import lax

BLK = 128
BLK_OWN = 128
CAP = 4
GCAP = 8
NBLK = 16384
N_DP = 128


def make_lists(key):
    base_key = jax.random.fold_in(key, 7177)
    keys = jax.random.split(base_key, 9)
    half_len = BLK_OWN // 2
    pair_count = N_DP // 2
    longest = BLK_OWN + half_len
    deltas = jax.random.randint(keys[0], (pair_count,), 0, half_len + 1)
    forced = jax.random.randint(keys[1], (), 0, pair_count)
    deltas = deltas.at[forced].set(half_len)
    lengths = jnp.concatenate([BLK_OWN + deltas, BLK_OWN - deltas]).astype(jnp.int32)
    lengths = jax.random.permutation(keys[2], lengths)
    starts = jnp.cumsum(lengths) - lengths
    positions = jnp.arange(longest, dtype=jnp.int32)
    gath_scores = jax.random.randint(keys[6], (N_DP, longest), 0, 65536) * longest + positions
    gath_scores = jnp.where(positions[None, :] < lengths[:, None], gath_scores, -1)
    gath_offsets = lax.top_k(gath_scores, GCAP)[1]
    gath_idx = (starts[:, None] + gath_offsets).astype(jnp.int32)
    low_count = GCAP - GCAP // 4
    gath_count = jax.random.randint(keys[7], (N_DP,), low_count, GCAP + 1)
    full_lister = jax.random.randint(keys[8], (), 0, N_DP)
    gath_count = gath_count.at[(full_lister + 1) % N_DP].set(low_count)
    gath_count = gath_count.at[full_lister].set(GCAP).astype(jnp.int32)
    list_pos = jnp.arange(GCAP, dtype=jnp.int32)
    sel_scores = jax.random.randint(keys[3], (N_DP, N_DP, GCAP), 0, 65536) * GCAP + list_pos
    sel_pick = lax.top_k(sel_scores, CAP)[1]
    gath_wide = jnp.broadcast_to(gath_idx[None, :, :], (N_DP, N_DP, GCAP))
    sel_idx = jnp.take_along_axis(gath_wide, sel_pick, axis=2).astype(jnp.int32)
    sel_count = jax.random.randint(keys[4], (N_DP, N_DP), 1, CAP + 1)
    full_owner = jax.random.randint(keys[5], (), 0, N_DP)
    sel_count = sel_count.at[:, full_owner].set(CAP).astype(jnp.int32)
    return (sel_idx, sel_count, gath_idx, gath_count)


def draw_sel_idx(key, part):
    return make_lists(key)[0]


def draw_sel_count(key, part):
    return make_lists(key)[1]


def draw_gath_idx(key, part):
    return make_lists(key)[2]


def draw_gath_count(key, part):
    return make_lists(key)[3]


def level_of(key, extent, shards, low, top_value):
    factor_of, own = 1.0, jax.random.fold_in(key, 6)
    for position, shards_of in shards:
        steps = jnp.exp(jax.random.uniform(jax.random.fold_in(own, position), (shards_of,), jnp.float32, low / len(shards), top_value / len(shards)))
        factor_of = factor_of * jnp.repeat(steps, extent[position] // shards_of).reshape([-1 if axis == position else 1 for axis in range(len(extent))])
    return factor_of


def normal_values(stream_key, extent, deviation, reach, pieces=(), held_as=jnp.bfloat16):
    values = jax.random.normal(stream_key, extent, jnp.float32) * deviation
    if len(pieces) > 0:
        values = level_of(stream_key, extent, pieces, -0.22, 0.18) * values
    return jnp.clip(values, min=-reach, max=reach).astype(held_as)


def setup_inputs(seed: int = 0) -> dict:
    arg_keys = jax.random.split(jax.random.key(seed), 9)
    gradient = normal_values(arg_keys[0], (N_DP, NBLK, BLK), 1.0, 6.0, ((0, 128),), jnp.float32)
    residual = normal_values(arg_keys[1], (N_DP, NBLK, BLK), 0.7, 5.0, ((0, 128),), jnp.float32)
    weights = normal_values(arg_keys[2], (NBLK, BLK), 1.0, 6.0, (), jnp.float32)
    momentum = normal_values(arg_keys[3], (NBLK, BLK), 1.0, 6.0, (), jnp.float32)
    sel_idx = draw_sel_idx(jax.random.fold_in(arg_keys[8], 71), 0)
    sel_count = draw_sel_count(jax.random.fold_in(arg_keys[8], 71), 0)
    gath_idx = draw_gath_idx(jax.random.fold_in(arg_keys[8], 71), 0)
    gath_count = draw_gath_count(jax.random.fold_in(arg_keys[8], 71), 0)
    return {"gradient": gradient, "residual": residual, "weights": weights, "momentum": momentum, "sel_idx": sel_idx, "sel_count": sel_count, "gath_idx": gath_idx, "gath_count": gath_count}


momentum_coef = 0.9
learning_rate = 0.05


def reference(gradient, residual, weights, momentum, sel_idx, sel_count, gath_idx, gath_count):
    accumulated = gradient + residual
    slot_ids = jnp.arange(CAP, dtype=jnp.int32)
    sel_valid = (slot_ids[None, None, :] < sel_count[:, :, None]).astype(jnp.float32)

    def add_source(running, inputs):
        source_acc, source_ids, source_valid = inputs
        flat_ids = source_ids.reshape(-1)
        rows_in = source_acc[flat_ids] * source_valid.reshape(-1, 1)
        return running.at[flat_ids].add(rows_in), None

    summed = lax.scan(add_source, jnp.zeros((NBLK, BLK), jnp.float32), (accumulated, sel_idx, sel_valid))[0]
    gath_slots = jnp.arange(GCAP, dtype=jnp.int32)
    gath_valid = (gath_slots[None, :] < gath_count[:, None]).astype(jnp.float32)
    listed = jnp.zeros((NBLK,), jnp.float32).at[gath_idx.reshape(-1)].max(gath_valid.reshape(-1))
    update = summed * listed[:, None]
    new_momentum = momentum_coef * momentum + update
    new_weights = weights - learning_rate * new_momentum

    def source_mask(source_ids, source_valid):
        return jnp.zeros((NBLK,), jnp.float32).at[source_ids.reshape(-1)].max(source_valid.reshape(-1))

    sel_mask = jax.vmap(source_mask)(sel_idx, sel_valid)
    new_residual = accumulated * (1.0 - sel_mask * listed[None, :])[:, :, None]
    return new_weights, new_momentum, new_residual
```

```python
import jax
import jax.numpy as jnp
from jax import lax
from jax.experimental import pallas as pl
from jax.experimental.pallas import tpu as pltpu
from jax.sharding import PartitionSpec as P

momentum_coef = 0.9
learning_rate = 0.05
F32 = jnp.float32
VMEM = pl.BlockSpec(memory_space=pltpu.VMEM)
HBM = pl.BlockSpec(memory_space=pltpu.HBM)
CHUNKS = 8
VMEM_ALL = 67_000_000


def cost(nbytes):
    return pl.CostEstimate(flops=0, transcendentals=0, bytes_accessed=nbytes)


def gather_rows(sel_ref, grad_ref, res_ref, out_ref, ids, buf, id_sem, sem):
    cap, owners = ids.shape
    rows = cap * owners
    copy = pltpu.make_async_copy(sel_ref.at[lax.axis_index("dp")], ids, id_sem)
    copy.start()
    copy.wait()

    def issue(o, carry):
        for c in range(cap):
            block = ids[c, o]
            slot = o * cap + c
            pltpu.make_async_copy(grad_ref.at[pl.ds(block, 1)], buf.at[0, pl.ds(slot, 1)], sem).start()
            pltpu.make_async_copy(res_ref.at[pl.ds(block, 1)], buf.at[1, pl.ds(slot, 1)], sem).start()
        return carry

    lax.fori_loop(0, owners, issue, 0, unroll=4)
    pltpu.make_async_copy(grad_ref.at[pl.ds(0, rows)], buf.at[0], sem).wait()
    pltpu.make_async_copy(res_ref.at[pl.ds(0, rows)], buf.at[1], sem).wait()
    out_ref[...] = buf[0] + buf[1]


def reduce_rows(hot_ref, rows_ref, after_ref, out_ref):
    del after_ref
    sums = jnp.dot(hot_ref[...], rows_ref[...], precision=lax.Precision.HIGHEST, preferred_element_type=F32)
    slots = sums.shape[0]
    copies = out_ref.shape[0] // slots
    out_ref[...] = jnp.broadcast_to(sums[None], (copies,) + sums.shape).reshape(out_ref.shape)


def residual_pass(
    sel_ref, scount_ref, gath_ref, gcount_ref, grad_ref, res_ref, after_ref, out_ref, ids_v, cnt_v, ids_s, a, b, in_sem, out_sem, sem
):
    del after_ref
    blocks = grad_ref.shape[0]
    step = blocks // CHUNKS
    me = lax.axis_index("dp")
    ins = []
    for k in range(CHUNKS):
        part = pl.ds(k * step, step)
        ins.append(
            (
                pltpu.make_async_copy(grad_ref.at[part], a.at[part], in_sem.at[0, k]),
                pltpu.make_async_copy(res_ref.at[part], b.at[part], in_sem.at[1, k]),
            )
        )
        ins[-1][0].start()
        ins[-1][1].start()
    first = pltpu.make_async_copy(sel_ref.at[me], ids_v, sem.at[0])
    second = pltpu.make_async_copy(scount_ref.at[pl.ds(me, 1)], cnt_v, sem.at[1])
    first.start()
    second.start()
    first.wait()
    second.wait()
    ids = ids_v[...]
    cap, owners = ids.shape
    sent = lax.broadcasted_iota(jnp.int32, (cap, owners), 0) < jnp.broadcast_to(cnt_v[...], (cap, owners))
    listed = jnp.zeros((cap, owners), jnp.bool_)
    for k in range(gath_ref.shape[0]):
        same = ids == jnp.broadcast_to(gath_ref[pl.ds(k, 1), :], (cap, owners))
        listed = listed | (same & (jnp.broadcast_to(gcount_ref[...], (cap, owners)) > k))
    ids_v[...] = jnp.where(sent & listed, ids, blocks)
    third = pltpu.make_async_copy(ids_v, ids_s, sem.at[0])
    third.start()
    third.wait()
    for k in range(CHUNKS):
        part = pl.ds(k * step, step)
        ins[k][0].wait()
        ins[k][1].wait()
        a[part, :] = a[part, :] + b[part, :]
    zero = jnp.zeros((1, a.shape[1]), F32)

    def clear(o, carry):
        for c in range(cap):
            a[pl.ds(ids_s[c, o], 1), :] = zero
        return carry

    lax.fori_loop(0, owners, clear, 0, unroll=4)
    outs = []
    for k in range(CHUNKS):
        part = pl.ds(k * step, step)
        outs.append(pltpu.make_async_copy(a.at[part], out_ref.at[part], out_sem.at[k]))
        outs[-1].start()
    for copy in outs:
        copy.wait()


def base_pass(gath_ref, w_ref, m_ref, after_ref, nw_ref, nm_ref, wrow_ref, mrow_ref, w, m, in_sem, out_sem):
    del after_ref
    blocks = w_ref.shape[0]
    step = blocks // CHUNKS
    list_len, owners = gath_ref.shape
    ins = []
    for k in range(CHUNKS):
        part = pl.ds(k * step, step)
        ins.append(
            (
                pltpu.make_async_copy(m_ref.at[part], m.at[part], in_sem.at[0, k]),
                pltpu.make_async_copy(w_ref.at[part], w.at[part], in_sem.at[1, k]),
            )
        )
        ins[-1][0].start()
        ins[-1][1].start()
    outs = []
    for k in range(CHUNKS):
        part = pl.ds(k * step, step)
        ins[k][0].wait()
        ins[k][1].wait()
        base = momentum_coef * m[part, :]
        m[part, :] = base
        w[part, :] = w[part, :] - learning_rate * base
        outs.append(pltpu.make_async_copy(m.at[part], nm_ref.at[part], out_sem.at[0, k]))
        outs.append(pltpu.make_async_copy(w.at[part], nw_ref.at[part], out_sem.at[1, k]))
        outs[-1].start()
        outs[-2].start()

    def take(o, carry):
        for k in range(list_len):
            block = gath_ref[k, o]
            slot = o * list_len + k
            mrow_ref[pl.ds(slot, 1), :] = m[pl.ds(block, 1), :]
            wrow_ref[pl.ds(slot, 1), :] = w[pl.ds(block, 1), :]
        return carry

    lax.fori_loop(0, owners, take, 0, unroll=2)
    for copy in outs:
        copy.wait()


def patch(gath_ref, u_ref, wrow_ref, mrow_ref, nw_in, nm_in, nw_ref, nm_ref, wrow, mrow, sem):
    rows = u_ref.shape[0]
    list_len, owners = gath_ref.shape
    u = u_ref[...]
    mrow[...] = mrow_ref[...] + u
    wrow[...] = wrow_ref[...] - learning_rate * u

    def issue(o, carry):
        for k in range(list_len):
            block = gath_ref[k, o]
            slot = o * list_len + k
            pltpu.make_async_copy(mrow.at[pl.ds(slot, 1)], nm_ref.at[pl.ds(block, 1)], sem.at[0]).start()
            pltpu.make_async_copy(wrow.at[pl.ds(slot, 1)], nw_ref.at[pl.ds(block, 1)], sem.at[1]).start()
        return carry

    lax.fori_loop(0, owners, issue, 0, unroll=2)
    pltpu.make_async_copy(mrow, nm_ref.at[pl.ds(0, rows)], sem.at[0]).wait()
    pltpu.make_async_copy(wrow, nw_ref.at[pl.ds(0, rows)], sem.at[1]).wait()


def local(gradient, residual, weights, momentum, sel_idx, sel_count, gath_idx, gath_count):
    me = lax.axis_index("dp")
    grad, res = gradient[0], residual[0]
    blocks, width = grad.shape
    owners, cap = sel_idx.shape[1:]
    list_len = gath_idx.shape[1]
    sel_t = jnp.transpose(sel_idx, (0, 2, 1))
    gath_t = jnp.transpose(gath_idx, (1, 0))
    smem = pl.BlockSpec(memory_space=pltpu.SMEM)
    full = jax.ShapeDtypeStruct((blocks, width), F32)
    dma = pltpu.SemaphoreType.DMA

    rows = pl.pallas_call(
        gather_rows,
        out_shape=jax.ShapeDtypeStruct((owners * cap, width), F32),
        in_specs=[HBM, HBM, HBM],
        out_specs=VMEM,
        scratch_shapes=[
            pltpu.SMEM((cap, owners), jnp.int32),
            pltpu.VMEM((2, owners * cap, width), F32),
            dma(()),
            dma(()),
        ],
        compiler_params=pltpu.CompilerParams(vmem_limit_bytes=VMEM_ALL),
        cost_estimate=cost(owners * cap * width * 8),
        name="gather_rows",
    )(sel_t, grad, res)
    got = lax.all_to_all(rows.reshape(owners, cap, width), "dp", 0, 0, tiled=True)

    mine = lax.dynamic_index_in_dim(sel_idx, me, 1, keepdims=False)
    mine_count = lax.dynamic_index_in_dim(sel_count, me, 1, keepdims=False)
    my_list = lax.dynamic_index_in_dim(gath_idx, me, 0, keepdims=False)
    my_listed = lax.dynamic_index_in_dim(gath_count, me, 0, keepdims=False)
    hot = (
        (mine[None] == my_list[:, None, None])
        & (jnp.arange(cap)[None, None, :] < mine_count[None, :, None])
        & (jnp.arange(list_len)[:, None, None] < my_listed)
    )
    hot = hot.astype(F32).reshape(list_len, owners * cap)

    new_residual = pl.pallas_call(
        residual_pass,
        out_shape=full,
        in_specs=[HBM, HBM, VMEM, VMEM, HBM, HBM, HBM],
        out_specs=HBM,
        scratch_shapes=[
            pltpu.VMEM((cap, owners), jnp.int32),
            pltpu.VMEM((1, owners), jnp.int32),
            pltpu.SMEM((cap, owners), jnp.int32),
            pltpu.VMEM((blocks + 8, width), F32),
            pltpu.VMEM((blocks, width), F32),
            dma((2, CHUNKS)),
            dma((CHUNKS,)),
            dma((2,)),
        ],
        cost_estimate=cost(blocks * width * 12),
        name="residual_pass",
    )(sel_t, sel_count, gath_t, gath_count.reshape(1, owners), grad, res, rows)

    shared = pl.pallas_call(
        reduce_rows,
        out_shape=jax.ShapeDtypeStruct((owners * list_len, width), F32),
        in_specs=[VMEM, VMEM, HBM],
        out_specs=VMEM,
        compiler_params=pltpu.CompilerParams(vmem_limit_bytes=VMEM_ALL),
        cost_estimate=cost(owners * list_len * width * 8),
        name="reduce_rows",
    )(hot, got.reshape(owners * cap, width), new_residual)
    sums = lax.all_to_all(shared.reshape(owners, list_len, width), "dp", 0, 0, tiled=True)

    listed_rows = jax.ShapeDtypeStruct((owners * list_len, width), F32)
    nw, nm, wrow, mrow = pl.pallas_call(
        base_pass,
        out_shape=(full, full, listed_rows, listed_rows),
        in_specs=[smem, HBM, HBM, HBM],
        out_specs=(HBM, HBM, VMEM, VMEM),
        scratch_shapes=[
            pltpu.VMEM((blocks, width), F32),
            pltpu.VMEM((blocks, width), F32),
            dma((2, CHUNKS)),
            dma((2, CHUNKS)),
        ],
        cost_estimate=cost(blocks * width * 16),
        name="base_pass",
    )(gath_t, weights, momentum, shared)

    new_weights, new_momentum = pl.pallas_call(
        patch,
        out_shape=(full, full),
        in_specs=[smem, VMEM, VMEM, VMEM, HBM, HBM],
        out_specs=(HBM, HBM),
        scratch_shapes=[
            pltpu.VMEM((owners * list_len, width), F32),
            pltpu.VMEM((owners * list_len, width), F32),
            dma((2,)),
        ],
        input_output_aliases={4: 0, 5: 1},
        compiler_params=pltpu.CompilerParams(vmem_limit_bytes=VMEM_ALL),
        cost_estimate=cost(owners * list_len * width * 16),
        name="patch",
    )(gath_t, sums.reshape(owners * list_len, width), wrow, mrow, nw, nm)
    return new_weights, new_momentum, new_residual[None]


def solution(mesh):
    placed = (P("dp", None, None), P("dp", None, None), P(), P(), P(), P(), P(), P())
    return jax.shard_map(
        local,
        mesh=mesh,
        in_specs=placed,
        out_specs=(P(), P(), P("dp", None, None)),
        check_vma=False,
    )
```

```python
import jax
import jax.numpy as jnp
from jax import lax
from jax.experimental import pallas as pl
from jax.experimental.pallas import tpu as pltpu
from jax.sharding import PartitionSpec as P

momentum_coef = 0.9
learning_rate = 0.05
F32 = jnp.float32
I32 = jnp.int32
VMEM = pl.BlockSpec(memory_space=pltpu.VMEM)
SMEM = pl.BlockSpec(memory_space=pltpu.SMEM)
HBM = pl.BlockSpec(memory_space=pltpu.HBM)
DMA = pltpu.SemaphoreType.DMA
EXACT = lax.Precision.HIGHEST
CHUNKS = 8
FRONT = 4
VMEM_ALL = 67_000_000


def cost(nbytes):
    return pl.CostEstimate(flops=0, transcendentals=0, bytes_accessed=nbytes)


def copy(src, dst, sem):
    return pltpu.make_async_copy(src, dst, sem)


def front(sel_ref, grad_ref, res_ref, rows_ref, nr_ref, ids, ids_v, pair, a, b, id_sem, row_sem, in_sem, out_sem):
    cap, owners = ids.shape
    step = grad_ref.shape[0] // CHUNKS
    bound = FRONT * step
    mine = sel_ref.at[pl.ds(lax.axis_index("dp") * cap, cap)]
    ids_copies = copy(mine, ids, id_sem.at[0]), copy(mine, ids_v, id_sem.at[1])
    for c in ids_copies:
        c.start()
    ins = []
    for i in range(FRONT):
        part = pl.ds(i * step, step)
        ins.append((copy(grad_ref.at[part], a.at[part], in_sem.at[0, i]), copy(res_ref.at[part], b.at[part], in_sem.at[1, i])))
        ins[-1][0].start()
        ins[-1][1].start(priority=1)
    for c in ids_copies:
        c.wait()
    top = jnp.max(ids_v[...], axis=0, keepdims=True)
    streamed = jnp.sum((top < bound).astype(F32)).astype(I32)

    def fetch(o, carry):
        theirs = [ids[c, o] for c in range(cap)]
        for c in range(cap):
            block, slot = pl.ds(theirs[c], 1), pl.ds(o * cap + c, 1)
            copy(grad_ref.at[block], pair.at[0, slot], row_sem).start()
            copy(res_ref.at[block], pair.at[1, slot], row_sem).start(priority=1)
        return carry

    lax.fori_loop(streamed, owners, fetch, 0)
    outs = []
    for i in range(FRONT):
        part = pl.ds(i * step, step)
        ins[i][0].wait()
        ins[i][1].wait()
        a[part, :] = a[part, :] + b[part, :]
        outs.append(copy(a.at[part], nr_ref.at[part], out_sem.at[i]))
        outs[-1].start()

    def pick(o, carry):
        theirs = [a[pl.ds(ids[c, o], 1), :] for c in range(cap)]
        for c in range(cap):
            rows_ref[pl.ds(o * cap + c, 1), :] = theirs[c]
        return carry

    lax.fori_loop(0, streamed, pick, 0)

    def land(o, carry):
        four = pl.ds(0, cap)
        copy(grad_ref.at[four], pair.at[0, four], row_sem).wait()
        copy(res_ref.at[four], pair.at[1, four], row_sem).wait()
        return carry

    lax.fori_loop(streamed, owners, land, 0)

    def add(o, carry):
        part = pl.ds(o * cap, cap)
        rows_ref[part, :] = pair[0, part, :] + pair[1, part, :]
        return carry

    lax.fori_loop(streamed, owners, add, 0)
    for c in outs:
        c.wait()


def middle(
    cap,
    sel_ref,
    scount_ref,
    gath_ref,
    gcount_ref,
    grad_ref,
    res_ref,
    nr_in,
    nr_ref,
    hot_ref,
    plan_ref,
    sel_v,
    scount_v,
    plan,
    a,
    b,
    idx_sem,
    in_sem,
    out_sem,
):
    del nr_in
    blocks = grad_ref.shape[0]
    step = blocks // CHUNKS
    base = FRONT * step
    me = lax.axis_index("dp")
    slots, owners = gath_ref.shape
    idx = copy(sel_ref, sel_v, idx_sem.at[0]), copy(scount_ref, scount_v, idx_sem.at[1])
    for c in idx:
        c.start()
    ins = []
    for i in range(CHUNKS - FRONT):
        part, here = pl.ds(base + i * step, step), pl.ds(i * step, step)
        ins.append((copy(grad_ref.at[part], a.at[here], in_sem.at[0, i]), copy(res_ref.at[part], b.at[here], in_sem.at[1, i])))
        ins[-1][0].start()
        ins[-1][1].start(priority=1)
    for c in idx:
        c.wait()

    lane = lax.broadcasted_iota(I32, (slots, owners), 1)
    gath = gath_ref[...]
    gcount = jnp.broadcast_to(gcount_ref[...], (slots, owners))
    listed = lax.broadcasted_iota(I32, (slots, owners), 0) < gcount
    ids = sel_v[pl.ds(me * cap, cap), :]
    count = jnp.broadcast_to(scount_v[pl.ds(me, 1), :], (cap, owners))
    sent = lax.broadcasted_iota(I32, (cap, owners), 0) < count
    hit = jnp.zeros((cap, owners), I32)
    for k in range(slots):
        same = (ids == jnp.broadcast_to(gath_ref[pl.ds(k, 1), :], (cap, owners))) & (gcount[:cap] > k)
        hit = hit + same.astype(I32)
    plan_ref[pl.ds(0, cap), :] = jnp.where(sent & (hit > 0), ids, blocks)
    edge = lax.broadcasted_iota(I32, (CHUNKS, owners), 0) * step
    top = jnp.broadcast_to(jnp.max(gath, axis=0, keepdims=True), (CHUNKS, owners))
    low = jnp.broadcast_to(jnp.min(gath, axis=0, keepdims=True), (CHUNKS, owners))
    first = jnp.sum((top < edge).astype(F32), axis=1, keepdims=True)
    last = jnp.sum((low < edge + step).astype(F32), axis=1, keepdims=True)
    plan_ref[pl.ds(8, CHUNKS), :] = jnp.broadcast_to(first, (CHUNKS, owners)).astype(I32)
    plan_ref[pl.ds(16, CHUNKS), :] = jnp.broadcast_to(last, (CHUNKS, owners)).astype(I32)
    to_smem = copy(plan_ref, plan, idx_sem.at[0])
    to_smem.start()

    mine = jnp.sum(jnp.where((lane == me) & listed, gath + 1, 0).astype(F32), axis=1, keepdims=True) - 1.0
    mine = jnp.where(mine < 0.0, -2.0, mine)
    pick = (lane == me).astype(F32)
    scount = scount_v[...]
    for c in range(cap):
        theirs = jnp.where(scount > c, sel_v[pl.ds(c, owners, stride=cap), :], -1).astype(F32)
        here = lax.dot_general(pick, theirs, (((1,), (1,)), ((), ())), precision=EXACT, preferred_element_type=F32)
        hot_ref[pl.ds(c * slots, slots), :] = (here == mine).astype(F32)
    to_smem.wait()

    zero = jnp.zeros((1, a.shape[1]), F32)
    outs = []
    for i in range(CHUNKS - FRONT):
        part, here = pl.ds(base + i * step, step), pl.ds(i * step, step)
        ins[i][0].wait()
        ins[i][1].wait()
        a[here, :] = a[here, :] + b[here, :]
        lo, hi = base + i * step, base + (i + 1) * step

        def clear(o, carry):
            for block in [plan[c, o] for c in range(cap)]:
                a[pl.ds(jnp.where((block >= lo) & (block < hi), block, blocks) - base, 1), :] = zero
            return carry

        lax.fori_loop(plan[8 + FRONT + i, 0], plan[16 + FRONT + i, 0], clear, 0)
        outs.append(copy(a.at[here], nr_ref.at[part], out_sem.at[i]))
        outs[-1].start()

    for c in outs:
        c.wait()


def reduce_rows(hot_ref, rows_ref, out_ref):
    owners = hot_ref.shape[1]
    cap = rows_ref.shape[0] // owners
    slots = hot_ref.shape[0] // cap
    sums = jnp.zeros((slots, rows_ref.shape[1]), F32)
    for c in range(cap):
        sums = sums + jnp.dot(
            hot_ref[pl.ds(c * slots, slots), :],
            rows_ref[pl.ds(c, owners, stride=cap), :],
            precision=EXACT,
            preferred_element_type=F32,
        )
    out_ref[...] = jnp.broadcast_to(sums[None], (owners,) + sums.shape).reshape(out_ref.shape)


def early(cap, plan, gath, w_ref, m_ref, nr_in, nw_ref, nm_ref, wrow_ref, mrow_ref, nr_ref, zeros, w, m, row_sem, in_sem, out_sem):
    del nr_in
    step = w_ref.shape[0] // CHUNKS
    slots = gath.shape[0]
    ins = []
    for i in range(CHUNKS):
        part = pl.ds(i * step, step)
        ins.append((copy(m_ref.at[part], m.at[part], in_sem.at[0, i]), copy(w_ref.at[part], w.at[part], in_sem.at[1, i])))
        ins[-1][0].start()
        ins[-1][1].start(priority=1)
    zeros[...] = jnp.zeros_like(zeros)

    def wipe(o, issued):
        for block in [plan[c, o] for c in range(cap)]:
            ours = block < FRONT * step

            @pl.when(ours)
            def _():
                copy(zeros.at[pl.ds(0, 1)], nr_ref.at[pl.ds(block, 1)], row_sem).start()

            issued = issued + ours.astype(I32)
        return issued

    issued = lax.fori_loop(0, plan[16 + FRONT - 1, 0], wipe, 0)
    outs = []
    for i in range(CHUNKS):
        part = pl.ds(i * step, step)
        ins[i][0].wait()
        ins[i][1].wait()
        base = momentum_coef * m[part, :]
        m[part, :] = base
        w[part, :] = w[part, :] - learning_rate * base
        outs.append(copy(m.at[part], nm_ref.at[part], out_sem.at[0, i]))
        outs.append(copy(w.at[part], nw_ref.at[part], out_sem.at[1, i]))
        outs[-2].start()
        outs[-1].start()

    def pick(o, carry):
        listed = [pl.ds(gath[k, o], 1) for k in range(slots)]
        mrows = [m[block, :] for block in listed]
        wrows = [w[block, :] for block in listed]
        for k in range(slots):
            slot = pl.ds(o * slots + k, 1)
            mrow_ref[slot, :] = mrows[k]
            wrow_ref[slot, :] = wrows[k]
        return carry

    lax.fori_loop(0, gath.shape[1], pick, 0)

    def land(o, carry):
        copy(zeros.at[pl.ds(0, 1)], nr_ref.at[pl.ds(0, 1)], row_sem).wait()
        return carry

    lax.fori_loop(0, issued, land, 0)
    for c in outs:
        c.wait()


def late(gath, count, u_ref, wrow_ref, mrow_ref, nw_in, nm_in, nw_ref, nm_ref, sums, wrow, mrow, list_sem, row_sem):
    del nw_in, nm_in
    slots, owners = gath.shape
    lists = copy(u_ref, sums, list_sem.at[0]), copy(mrow_ref, mrow, list_sem.at[1]), copy(wrow_ref, wrow, list_sem.at[2])
    for c in lists:
        c.start()
    for c in lists:
        c.wait()

    def patch(o, issued):
        part = pl.ds(pl.multiple_of(o * slots, slots), slots)
        mrow[part, :] = mrow[part, :] + sums[part, :]
        wrow[part, :] = wrow[part, :] - learning_rate * sums[part, :]
        used = count[0, o]
        listed = [gath[k, o] for k in range(slots)]
        for k in range(slots):

            @pl.when(k < used)
            def _():
                slot, block = pl.ds(o * slots + k, 1), pl.ds(listed[k], 1)
                copy(mrow.at[slot], nm_ref.at[block], row_sem.at[0]).start()
                copy(wrow.at[slot], nw_ref.at[block], row_sem.at[1]).start()

        return issued + used

    issued = lax.fori_loop(0, owners, patch, jnp.int32(0))
    size = slots * owners
    while size:
        part = pl.ds(0, size)

        @pl.when((issued & size) != 0)
        def _():
            copy(mrow.at[part], nm_ref.at[part], row_sem.at[0]).wait()
            copy(wrow.at[part], nw_ref.at[part], row_sem.at[1]).wait()

        size //= 2


def local(gradient, residual, weights, momentum, sel_idx, sel_count, gath_idx, gath_count):
    grad, res = gradient[0], residual[0]
    blocks, width = grad.shape
    owners, cap = sel_idx.shape[1:]
    slots = gath_idx.shape[1]
    step = blocks // CHUNKS
    sel = jnp.transpose(sel_idx, (0, 2, 1)).reshape(owners * cap, owners)
    gath = jnp.transpose(gath_idx, (1, 0))
    full = jax.ShapeDtypeStruct((blocks, width), F32)
    listed_rows = jax.ShapeDtypeStruct((owners * slots, width), F32)
    params = pltpu.CompilerParams(vmem_limit_bytes=VMEM_ALL)

    rows, nr = pl.pallas_call(
        front,
        out_shape=(jax.ShapeDtypeStruct((owners * cap, width), F32), full),
        in_specs=[HBM, HBM, HBM],
        out_specs=(VMEM, HBM),
        scratch_shapes=[
            pltpu.SMEM((cap, owners), I32),
            pltpu.VMEM((cap, owners), I32),
            pltpu.VMEM((2, owners * cap, width), F32),
            pltpu.VMEM((FRONT * step, width), F32),
            pltpu.VMEM((FRONT * step, width), F32),
            DMA((2,)),
            DMA(()),
            DMA((2, FRONT)),
            DMA((FRONT,)),
        ],
        compiler_params=params,
        cost_estimate=cost(FRONT * step * width * 12),
        name="front",
    )(sel, grad, res)
    got = lax.all_to_all(rows.reshape(owners, cap, width), "dp", 0, 0, tiled=True)

    rest = (CHUNKS - FRONT) * step
    nr, hot, plan = pl.pallas_call(
        lambda *refs: middle(cap, *refs),
        out_shape=(full, jax.ShapeDtypeStruct((cap * slots, owners), F32), jax.ShapeDtypeStruct((24, owners), I32)),
        in_specs=[HBM, HBM, VMEM, VMEM, HBM, HBM, HBM],
        out_specs=(HBM, VMEM, VMEM),
        scratch_shapes=[
            pltpu.VMEM((owners * cap, owners), I32),
            pltpu.VMEM((owners, owners), I32),
            pltpu.SMEM((24, owners), I32),
            pltpu.VMEM((rest + 8, width), F32),
            pltpu.VMEM((rest, width), F32),
            DMA((2,)),
            DMA((2, CHUNKS - FRONT)),
            DMA((CHUNKS - FRONT,)),
        ],
        input_output_aliases={6: 0},
        compiler_params=params,
        cost_estimate=cost(rest * width * 12),
        name="middle",
    )(sel, sel_count, gath, gath_count.reshape(1, owners), grad, res, nr)

    shared = pl.pallas_call(
        reduce_rows,
        out_shape=listed_rows,
        in_specs=[VMEM, VMEM],
        out_specs=VMEM,
        compiler_params=params,
        cost_estimate=cost(owners * slots * width * 8),
        name="reduce_rows",
    )(hot, got.reshape(owners * cap, width))
    sums = lax.all_to_all(shared.reshape(owners, slots, width), "dp", 0, 0, tiled=True)

    nw, nm, wrow, mrow, new_residual = pl.pallas_call(
        lambda *refs: early(cap, *refs),
        out_shape=(full, full, listed_rows, listed_rows, full),
        in_specs=[SMEM, SMEM, HBM, HBM, HBM],
        out_specs=(HBM, HBM, VMEM, VMEM, HBM),
        scratch_shapes=[
            pltpu.VMEM((8, width), F32),
            pltpu.VMEM((blocks, width), F32),
            pltpu.VMEM((blocks, width), F32),
            DMA(()),
            DMA((2, CHUNKS)),
            DMA((2, CHUNKS)),
        ],
        input_output_aliases={4: 4},
        compiler_params=params,
        cost_estimate=cost(blocks * width * 16),
        name="early",
    )(plan, gath, weights, momentum, nr)

    new_weights, new_momentum = pl.pallas_call(
        late,
        out_shape=(full, full),
        in_specs=[SMEM, SMEM, HBM, HBM, HBM, HBM, HBM],
        out_specs=(HBM, HBM),
        scratch_shapes=[
            pltpu.VMEM((owners * slots, width), F32),
            pltpu.VMEM((owners * slots, width), F32),
            pltpu.VMEM((owners * slots, width), F32),
            DMA((3,)),
            DMA((2,)),
        ],
        input_output_aliases={5: 0, 6: 1},
        compiler_params=params,
        cost_estimate=cost(owners * slots * width * 20),
        name="late",
    )(gath, gath_count.reshape(1, owners), sums.reshape(owners * slots, width), wrow, mrow, nw, nm)
    return new_weights, new_momentum, new_residual[None]


def solution(mesh):
    placed = (P("dp", None, None), P("dp", None, None), P(), P(), P(), P(), P(), P())
    return jax.shard_map(
        local,
        mesh=mesh,
        in_specs=placed,
        out_specs=(P(), P(), P("dp", None, None)),
        check_vma=False,
    )
```

```python
import jax
import jax.numpy as jnp
from jax import lax
from jax.experimental import pallas as pl
from jax.experimental.pallas import tpu as pltpu
from jax.sharding import PartitionSpec as P

momentum_coef = 0.9
learning_rate = 0.05
F32 = jnp.float32
I32 = jnp.int32
VMEM = pl.BlockSpec(memory_space=pltpu.VMEM)
HBM = pl.BlockSpec(memory_space=pltpu.HBM)
DMA = pltpu.SemaphoreType.DMA
EXACT = lax.Precision.HIGHEST
CHUNKS = 8
VMEM_ALL = 67_000_000


def cost(nbytes):
    return pl.CostEstimate(flops=0, transcendentals=0, bytes_accessed=nbytes)


def copy(src, dst, sem):
    return pltpu.make_async_copy(src, dst, sem)


def front(sel_ref, grad_ref, res_ref, rows_ref, ids, pair, id_sem, row_sem):
    cap, owners = ids.shape
    mine = copy(sel_ref.at[pl.ds(lax.axis_index("dp") * cap, cap)], ids, id_sem)
    mine.start()
    mine.wait()

    def fetch(o, carry):
        theirs = [ids[c, o] for c in range(cap)]
        for c in range(cap):
            block, slot = pl.ds(theirs[c], 1), pl.ds(o * cap + c, 1)
            copy(grad_ref.at[block], pair.at[0, slot], row_sem.at[0]).start()
            copy(res_ref.at[block], pair.at[1, slot], row_sem.at[1]).start(priority=1)
        return carry

    lax.fori_loop(0, owners, fetch, 0, unroll=2)
    every = pl.ds(0, cap * owners)
    copy(grad_ref.at[every], pair.at[0], row_sem.at[0]).wait()
    copy(res_ref.at[every], pair.at[1], row_sem.at[1]).wait()
    rows_ref[...] = pair[0] + pair[1]


def middle(
    cap,
    sel_ref,
    scount_ref,
    gath_hbm,
    gcount_hbm,
    grad_ref,
    res_ref,
    nr_ref,
    hot_hbm,
    plan_hbm,
    sel_v,
    scount_v,
    gath_ref,
    gcount_ref,
    hot_ref,
    plan_ref,
    plan,
    a,
    b,
    idx_sem,
    in_sem,
    out_sem,
):
    blocks = grad_ref.shape[0]
    step = blocks // CHUNKS
    me = lax.axis_index("dp")
    slots, owners = gath_ref.shape
    idx = (
        copy(gath_hbm, gath_ref, idx_sem.at[2]),
        copy(gcount_hbm, gcount_ref, idx_sem.at[3]),
        copy(scount_ref, scount_v, idx_sem.at[1]),
        copy(sel_ref, sel_v, idx_sem.at[0]),
    )
    for c in idx:
        c.start()
    ins = []
    for i in range(CHUNKS):
        part = pl.ds(i * step, step)
        ins.append((copy(grad_ref.at[part], a.at[part], in_sem.at[0, i]), copy(res_ref.at[part], b.at[part], in_sem.at[1, i])))
        ins[-1][0].start()
        ins[-1][1].start(priority=1)
    for c in idx:
        c.wait()

    lane = lax.broadcasted_iota(I32, (slots, owners), 1)
    gath = gath_ref[...]
    gcount = jnp.broadcast_to(gcount_ref[...], (slots, owners))
    listed = lax.broadcasted_iota(I32, (slots, owners), 0) < gcount
    ids = sel_v[pl.ds(me * cap, cap), :]
    count = jnp.broadcast_to(scount_v[pl.ds(me, 1), :], (cap, owners))
    sent = lax.broadcasted_iota(I32, (cap, owners), 0) < count
    hit = jnp.zeros((cap, owners), I32)
    for k in range(slots):
        same = (ids == jnp.broadcast_to(gath_ref[pl.ds(k, 1), :], (cap, owners))) & (gcount[:cap] > k)
        hit = hit + same.astype(I32)
    plan_ref[pl.ds(0, cap), :] = jnp.where(sent & (hit > 0), ids, blocks)
    edge = lax.broadcasted_iota(I32, (CHUNKS, owners), 0) * step
    top = jnp.broadcast_to(jnp.max(gath, axis=0, keepdims=True), (CHUNKS, owners))
    low = jnp.broadcast_to(jnp.min(gath, axis=0, keepdims=True), (CHUNKS, owners))
    first = jnp.sum((top < edge).astype(F32), axis=1, keepdims=True)
    last = jnp.sum((low < edge + step).astype(F32), axis=1, keepdims=True)
    plan_ref[pl.ds(8, CHUNKS), :] = jnp.broadcast_to(first, (CHUNKS, owners)).astype(I32)
    plan_ref[pl.ds(16, CHUNKS), :] = jnp.broadcast_to(last, (CHUNKS, owners)).astype(I32)
    to_smem = copy(plan_ref, plan, idx_sem.at[0])
    to_smem.start()

    mine = jnp.sum(jnp.where((lane == me) & listed, gath + 1, 0).astype(F32), axis=1, keepdims=True) - 1.0
    mine = jnp.where(mine < 0.0, -2.0, mine)
    pick = (lane == me).astype(F32)
    scount = scount_v[...]
    for c in range(cap):
        theirs = jnp.where(scount > c, sel_v[pl.ds(c, owners, stride=cap), :], -1).astype(F32)
        here = lax.dot_general(pick, theirs, (((1,), (1,)), ((), ())), precision=EXACT, preferred_element_type=F32)
        hot_ref[pl.ds(c * slots, slots), :] = (here == mine).astype(F32)
    to_smem.wait()
    outs = [copy(hot_ref, hot_hbm, idx_sem.at[2]), copy(plan_ref, plan_hbm, idx_sem.at[3])]
    for c in outs:
        c.start()
    zero = jnp.zeros((1, a.shape[1]), F32)
    for i in range(CHUNKS):
        part = pl.ds(i * step, step)
        ins[i][0].wait()
        ins[i][1].wait()
        a[part, :] = a[part, :] + b[part, :]
        lo, hi = i * step, (i + 1) * step

        def clear(o, carry):
            for block in [plan[c, o] for c in range(cap)]:
                a[pl.ds(jnp.where((block >= lo) & (block < hi), block, blocks), 1), :] = zero
            return carry

        lax.fori_loop(plan[8 + i, 0], plan[16 + i, 0], clear, 0)
        outs.append(copy(a.at[part], nr_ref.at[part], out_sem.at[i]))
        outs[-1].start()

    for c in outs:
        c.wait()


def reduce_rows(hot_ref, rows_ref, out_ref):
    owners = hot_ref.shape[1]
    cap = rows_ref.shape[0] // owners
    slots = hot_ref.shape[0] // cap
    sums = jnp.zeros((slots, rows_ref.shape[1]), F32)
    for c in range(cap):
        sums = sums + jnp.dot(
            hot_ref[pl.ds(c * slots, slots), :],
            rows_ref[pl.ds(c, owners, stride=cap), :],
            precision=EXACT,
            preferred_element_type=F32,
        )
    out_ref[...] = jnp.broadcast_to(sums[None], (owners,) + sums.shape).reshape(out_ref.shape)


def early(gath_ref, plan_ref, w_ref, m_ref, nw_ref, nm_ref, wrow_ref, mrow_ref, gath, plan, wrow, mrow, w, m, idx_sem, in_sem, out_sem):
    step = w_ref.shape[0] // CHUNKS
    slots, owners = gath.shape
    idx = copy(gath_ref, gath, idx_sem.at[0]), copy(plan_ref, plan, idx_sem.at[1])
    for c in idx:
        c.start()
    ins = []
    for i in range(CHUNKS):
        part = pl.ds(i * step, step)
        ins.append((copy(m_ref.at[part], m.at[part], in_sem.at[0, i]), copy(w_ref.at[part], w.at[part], in_sem.at[1, i])))
        ins[-1][0].start()
        ins[-1][1].start(priority=1)
    for c in idx:
        c.wait()

    def pick(o, carry):
        listed = [pl.ds(gath[k, o], 1) for k in range(slots)]
        mrows = [m[block, :] for block in listed]
        wrows = [w[block, :] for block in listed]
        for k in range(slots):
            slot = pl.ds(o * slots + k, 1)
            mrow[slot, :] = mrows[k]
            wrow[slot, :] = wrows[k]
        return carry

    outs = []
    done = 0
    for i in range(CHUNKS):
        part = pl.ds(i * step, step)
        ins[i][0].wait()
        ins[i][1].wait()
        base = momentum_coef * m[part, :]
        m[part, :] = base
        w[part, :] = w[part, :] - learning_rate * base
        outs.append(copy(m.at[part], nm_ref.at[part], out_sem.at[0, i]))
        outs.append(copy(w.at[part], nw_ref.at[part], out_sem.at[1, i]))
        outs[-2].start()
        outs[-1].start()
        below = plan[8 + i + 1, 0] if i + 1 < CHUNKS else owners
        lax.fori_loop(done, below, pick, 0)
        done = below
    outs.append(copy(mrow, mrow_ref, idx_sem.at[0]))
    outs.append(copy(wrow, wrow_ref, idx_sem.at[1]))
    outs[-2].start()
    outs[-1].start()
    for c in outs:
        c.wait()


def late(gath_ref, count_ref, u_ref, wrow_ref, mrow_ref, nw_in, nm_in, nw_ref, nm_ref, gath, count, sums, wrow, mrow, list_sem, row_sem):
    del nw_in, nm_in
    slots, owners = gath.shape
    lists = (
        copy(gath_ref, gath, list_sem.at[3]),
        copy(count_ref, count, list_sem.at[4]),
        copy(u_ref, sums, list_sem.at[0]),
        copy(mrow_ref, mrow, list_sem.at[1]),
        copy(wrow_ref, wrow, list_sem.at[2]),
    )
    for c, thread in zip(lists, (0, 1, 0, 1, 0)):
        c.start(priority=thread)
    for c in lists:
        c.wait()

    def patch(o, issued):
        part = pl.ds(pl.multiple_of(o * slots, slots), slots)
        mrow[part, :] = mrow[part, :] + sums[part, :]
        wrow[part, :] = wrow[part, :] - learning_rate * sums[part, :]
        used = count[0, o]
        listed = [gath[k, o] for k in range(slots)]
        for k in range(slots):

            @pl.when(k < used)
            def _():
                slot, block = pl.ds(o * slots + k, 1), pl.ds(listed[k], 1)
                copy(mrow.at[slot], nm_ref.at[block], row_sem.at[0]).start()
                copy(wrow.at[slot], nw_ref.at[block], row_sem.at[1]).start(priority=1)

        return issued + used

    issued = lax.fori_loop(0, owners, patch, jnp.int32(0))
    size = slots * owners
    while size:
        part = pl.ds(0, size)

        @pl.when((issued & size) != 0)
        def _():
            copy(mrow.at[part], nm_ref.at[part], row_sem.at[0]).wait()
            copy(wrow.at[part], nw_ref.at[part], row_sem.at[1]).wait()

        size //= 2


def local(gradient, residual, weights, momentum, sel_idx, sel_count, gath_idx, gath_count):
    grad, res = gradient[0], residual[0]
    blocks, width = grad.shape
    owners, cap = sel_idx.shape[1:]
    slots = gath_idx.shape[1]
    sel = jnp.transpose(sel_idx, (0, 2, 1)).reshape(owners * cap, owners)
    gath = jnp.transpose(gath_idx, (1, 0))
    full = jax.ShapeDtypeStruct((blocks, width), F32)
    listed_rows = jax.ShapeDtypeStruct((owners * slots, width), F32)
    params = pltpu.CompilerParams(vmem_limit_bytes=VMEM_ALL)

    rows = pl.pallas_call(
        front,
        out_shape=jax.ShapeDtypeStruct((owners * cap, width), F32),
        in_specs=[HBM, HBM, HBM],
        out_specs=VMEM,
        scratch_shapes=[
            pltpu.SMEM((cap, owners), I32),
            pltpu.VMEM((2, owners * cap, width), F32),
            DMA(()),
            DMA((2,)),
        ],
        compiler_params=params,
        cost_estimate=cost(owners * cap * width * 12),
        name="front",
    )(sel, grad, res)
    got = lax.all_to_all(rows.reshape(owners, cap, width), "dp", 0, 0, tiled=True)

    new_residual, hot, plan = pl.pallas_call(
        lambda *refs: middle(cap, *refs),
        out_shape=(full, jax.ShapeDtypeStruct((cap * slots, owners), F32), jax.ShapeDtypeStruct((24, owners), I32)),
        in_specs=[HBM] * 6,
        out_specs=(HBM, HBM, HBM),
        scratch_shapes=[
            pltpu.VMEM((owners * cap, owners), I32),
            pltpu.VMEM((owners, owners), I32),
            pltpu.VMEM((slots, owners), I32),
            pltpu.VMEM((1, owners), I32),
            pltpu.VMEM((cap * slots, owners), F32),
            pltpu.VMEM((24, owners), I32),
            pltpu.SMEM((24, owners), I32),
            pltpu.VMEM((blocks + 8, width), F32),
            pltpu.VMEM((blocks, width), F32),
            DMA((4,)),
            DMA((2, CHUNKS)),
            DMA((CHUNKS,)),
        ],
        compiler_params=pltpu.CompilerParams(vmem_limit_bytes=60_000_000),
        cost_estimate=cost(blocks * width * 12),
        name="middle",
    )(sel, sel_count, gath, gath_count.reshape(1, owners), grad, res)

    shared = pl.pallas_call(
        reduce_rows,
        out_shape=listed_rows,
        in_specs=[VMEM, VMEM],
        out_specs=VMEM,
        compiler_params=pltpu.CompilerParams(vmem_limit_bytes=8 << 20),
        cost_estimate=cost(owners * slots * width * 8),
        name="reduce_rows",
    )(hot, got.reshape(owners * cap, width))
    sums = lax.all_to_all(shared.reshape(owners, slots, width), "dp", 0, 0, tiled=True)

    nw, nm, wrow, mrow = pl.pallas_call(
        early,
        out_shape=(full, full, listed_rows, listed_rows),
        in_specs=[HBM] * 4,
        out_specs=(HBM,) * 4,
        scratch_shapes=[
            pltpu.SMEM((slots, owners), I32),
            pltpu.SMEM((24, owners), I32),
            pltpu.VMEM((owners * slots, width), F32),
            pltpu.VMEM((owners * slots, width), F32),
            pltpu.VMEM((blocks, width), F32),
            pltpu.VMEM((blocks, width), F32),
            DMA((2,)),
            DMA((2, CHUNKS)),
            DMA((2, CHUNKS)),
        ],
        compiler_params=params,
        cost_estimate=cost(blocks * width * 16),
        name="early",
    )(gath, plan, weights, momentum)

    new_weights, new_momentum = pl.pallas_call(
        late,
        out_shape=(full, full),
        in_specs=[HBM] * 7,
        out_specs=(HBM, HBM),
        scratch_shapes=[
            pltpu.SMEM((slots, owners), I32),
            pltpu.SMEM((1, owners), I32),
            pltpu.VMEM((owners * slots, width), F32),
            pltpu.VMEM((owners * slots, width), F32),
            pltpu.VMEM((owners * slots, width), F32),
            DMA((5,)),
            DMA((2,)),
        ],
        input_output_aliases={5: 0, 6: 1},
        compiler_params=params,
        cost_estimate=cost(owners * slots * width * 20),
        name="late",
    )(gath, gath_count.reshape(1, owners), sums.reshape(owners * slots, width), wrow, mrow, nw, nm)
    return new_weights, new_momentum, new_residual[None]


def solution(mesh):
    placed = (P("dp", None, None), P("dp", None, None), P(), P(), P(), P(), P(), P())
    return jax.shard_map(
        local,
        mesh=mesh,
        in_specs=placed,
        out_specs=(P(), P(), P("dp", None, None)),
        check_vma=False,
    )
```

```python
import jax
import jax.numpy as jnp
from jax import lax
from jax.experimental import pallas as pl
from jax.experimental.pallas import tpu as pltpu
from jax.sharding import PartitionSpec as P

momentum_coef = 0.9
learning_rate = 0.05
F32 = jnp.float32
I32 = jnp.int32
VMEM = pl.BlockSpec(memory_space=pltpu.VMEM)
HBM = pl.BlockSpec(memory_space=pltpu.HBM)
DMA = pltpu.SemaphoreType.DMA
EXACT = lax.Precision.HIGHEST
CHUNKS = 8
VMEM_ALL = 67_000_000


def cost(nbytes):
    return pl.CostEstimate(flops=0, transcendentals=0, bytes_accessed=nbytes)


def copy(src, dst, sem):
    return pltpu.make_async_copy(src, dst, sem)


def front(sel_ref, grad_ref, res_ref, rows_ref, ids, pair, id_sem, row_sem):
    cap, owners = ids.shape
    mine = copy(sel_ref.at[pl.ds(lax.axis_index("dp") * cap, cap)], ids, id_sem)
    mine.start()
    mine.wait()

    def fetch(o, carry):
        theirs = [ids[c, o] for c in range(cap)]
        for c in range(cap):
            block, slot = pl.ds(theirs[c], 1), pl.ds(o * cap + c, 1)
            copy(grad_ref.at[block], pair.at[0, slot], row_sem.at[0]).start()
            copy(res_ref.at[block], pair.at[1, slot], row_sem.at[1]).start(priority=1)
        return carry

    lax.fori_loop(0, owners, fetch, 0, unroll=2)
    every = pl.ds(0, cap * owners)
    copy(grad_ref.at[every], pair.at[0], row_sem.at[0]).wait()
    copy(res_ref.at[every], pair.at[1], row_sem.at[1]).wait()
    rows_ref[...] = pair[0] + pair[1]


def middle(
    cap,
    sel_ref,
    scount_ref,
    gath_hbm,
    gcount_hbm,
    grad_ref,
    res_ref,
    nr_ref,
    hot_hbm,
    plan_hbm,
    sel_v,
    scount_v,
    gath_ref,
    gcount_ref,
    hot_ref,
    plan_ref,
    plan,
    a,
    b,
    idx_sem,
    in_sem,
    out_sem,
):
    blocks = grad_ref.shape[0]
    step = blocks // CHUNKS
    me = lax.axis_index("dp")
    slots, owners = gath_ref.shape
    idx = (
        copy(gath_hbm, gath_ref, idx_sem.at[2]),
        copy(gcount_hbm, gcount_ref, idx_sem.at[3]),
        copy(scount_ref, scount_v, idx_sem.at[1]),
        copy(sel_ref, sel_v, idx_sem.at[0]),
    )
    for c in idx:
        c.start()
    ins = []
    for i in range(CHUNKS):
        part = pl.ds(i * step, step)
        ins.append((copy(grad_ref.at[part], a.at[part], in_sem.at[0, i]), copy(res_ref.at[part], b.at[part], in_sem.at[1, i])))
        ins[-1][0].start()
        ins[-1][1].start(priority=1)
    for c in idx:
        c.wait()

    lane = lax.broadcasted_iota(I32, (slots, owners), 1)
    gath = gath_ref[...]
    gcount = jnp.broadcast_to(gcount_ref[...], (slots, owners))
    listed = lax.broadcasted_iota(I32, (slots, owners), 0) < gcount
    ids = sel_v[pl.ds(me * cap, cap), :]
    count = jnp.broadcast_to(scount_v[pl.ds(me, 1), :], (cap, owners))
    sent = lax.broadcasted_iota(I32, (cap, owners), 0) < count
    hit = jnp.zeros((cap, owners), I32)
    for k in range(slots):
        same = (ids == jnp.broadcast_to(gath_ref[pl.ds(k, 1), :], (cap, owners))) & (gcount[:cap] > k)
        hit = hit + same.astype(I32)
    plan_ref[pl.ds(0, cap), :] = jnp.where(sent & (hit > 0), ids, blocks)
    edge = lax.broadcasted_iota(I32, (CHUNKS, owners), 0) * step
    top = jnp.broadcast_to(jnp.max(gath, axis=0, keepdims=True), (CHUNKS, owners))
    low = jnp.broadcast_to(jnp.min(gath, axis=0, keepdims=True), (CHUNKS, owners))
    first = jnp.sum((top < edge).astype(F32), axis=1, keepdims=True)
    last = jnp.sum((low < edge + step).astype(F32), axis=1, keepdims=True)
    plan_ref[pl.ds(8, CHUNKS), :] = jnp.broadcast_to(first, (CHUNKS, owners)).astype(I32)
    plan_ref[pl.ds(16, CHUNKS), :] = jnp.broadcast_to(last, (CHUNKS, owners)).astype(I32)
    to_smem = copy(plan_ref, plan, idx_sem.at[0])
    to_smem.start()

    mine = jnp.sum(jnp.where((lane == me) & listed, gath + 1, 0).astype(F32), axis=1, keepdims=True) - 1.0
    mine = jnp.where(mine < 0.0, -2.0, mine)
    pick = (lane == me).astype(F32)
    scount = scount_v[...]
    for c in range(cap):
        theirs = jnp.where(scount > c, sel_v[pl.ds(c, owners, stride=cap), :], -1).astype(F32)
        here = lax.dot_general(pick, theirs, (((1,), (1,)), ((), ())), precision=EXACT, preferred_element_type=F32)
        hot_ref[pl.ds(c * slots, slots), :] = (here == mine).astype(F32)
    to_smem.wait()
    outs = [copy(hot_ref, hot_hbm, idx_sem.at[2]), copy(plan_ref, plan_hbm, idx_sem.at[3])]
    for c in outs:
        c.start()
    zero = jnp.zeros((1, a.shape[1]), F32)
    for i in range(CHUNKS):
        part = pl.ds(i * step, step)
        ins[i][0].wait()
        ins[i][1].wait()
        a[part, :] = a[part, :] + b[part, :]
        lo, hi = i * step, (i + 1) * step

        def clear(o, carry):
            for block in [plan[c, o] for c in range(cap)]:
                a[pl.ds(jnp.where((block >= lo) & (block < hi), block, blocks), 1), :] = zero
            return carry

        lax.fori_loop(plan[8 + i, 0], plan[16 + i, 0], clear, 0)
        outs.append(copy(a.at[part], nr_ref.at[part], out_sem.at[i]))
        outs[-1].start()

    for c in outs:
        c.wait()


def reduce_rows(hot_ref, rows_ref, out_ref):
    owners = hot_ref.shape[1]
    cap = rows_ref.shape[0] // owners
    slots = hot_ref.shape[0] // cap
    sums = jnp.zeros((slots, rows_ref.shape[1]), F32)
    for c in range(cap):
        sums = sums + jnp.dot(
            hot_ref[pl.ds(c * slots, slots), :],
            rows_ref[pl.ds(c, owners, stride=cap), :],
            precision=EXACT,
            preferred_element_type=F32,
        )
    out_ref[...] = jnp.broadcast_to(sums[None], (owners,) + sums.shape).reshape(out_ref.shape)


def early(gath_ref, plan_ref, w_ref, m_ref, nw_ref, nm_ref, wrow_ref, mrow_ref, gath, plan, wrow, mrow, w, m, idx_sem, in_sem, out_sem):
    step = w_ref.shape[0] // CHUNKS
    slots, owners = gath.shape
    idx = copy(gath_ref, gath, idx_sem.at[0]), copy(plan_ref, plan, idx_sem.at[1])
    for c in idx:
        c.start()
    ins = []
    for i in range(CHUNKS):
        part = pl.ds(i * step, step)
        ins.append((copy(m_ref.at[part], m.at[part], in_sem.at[0, i]), copy(w_ref.at[part], w.at[part], in_sem.at[1, i])))
        ins[-1][0].start()
        ins[-1][1].start(priority=1)
    for c in idx:
        c.wait()

    def pick(o, carry):
        listed = [pl.ds(gath[k, o], 1) for k in range(slots)]
        mrows = [m[block, :] for block in listed]
        wrows = [w[block, :] for block in listed]
        for k in range(slots):
            slot = pl.ds(o * slots + k, 1)
            mrow[slot, :] = mrows[k]
            wrow[slot, :] = wrows[k]
        return carry

    outs = []
    done = 0
    for i in range(CHUNKS):
        part = pl.ds(i * step, step)
        ins[i][0].wait()
        ins[i][1].wait()
        base = momentum_coef * m[part, :]
        m[part, :] = base
        w[part, :] = w[part, :] - learning_rate * base
        outs.append(copy(m.at[part], nm_ref.at[part], out_sem.at[0, i]))
        outs.append(copy(w.at[part], nw_ref.at[part], out_sem.at[1, i]))
        outs[-2].start()
        outs[-1].start()
        below = plan[8 + i + 1, 0] if i + 1 < CHUNKS else owners
        lax.fori_loop(done, below, pick, 0)
        done = below
    outs.append(copy(mrow, mrow_ref, idx_sem.at[0]))
    outs.append(copy(wrow, wrow_ref, idx_sem.at[1]))
    outs[-2].start()
    outs[-1].start()
    for c in outs:
        c.wait()


def late(gath_ref, count_ref, u_ref, wrow_ref, mrow_ref, nw_in, nm_in, nw_ref, nm_ref, gath, count, sums, wrow, mrow, list_sem, row_sem):
    del nw_in, nm_in
    slots, owners = gath.shape
    half = owners // 2
    lists = [copy(gath_ref, gath, list_sem.at[0, 3]), copy(count_ref, count, list_sem.at[0, 4])]
    later = []
    for i, group in enumerate((lists, later)):
        part = pl.ds(i * half * slots, half * slots)
        for j, (src, dst) in enumerate(((u_ref, sums), (mrow_ref, mrow), (wrow_ref, wrow))):
            group.append(copy(src.at[part], dst.at[part], list_sem.at[i, j]))
    for j, c in enumerate(lists + later):
        c.start(priority=j % 2)
    for c in lists:
        c.wait()

    def patch(o, issued):
        part = pl.ds(pl.multiple_of(o * slots, slots), slots)
        mrow[part, :] = mrow[part, :] + sums[part, :]
        wrow[part, :] = wrow[part, :] - learning_rate * sums[part, :]
        used = count[0, o]
        listed = [gath[k, o] for k in range(slots)]
        for k in range(slots):

            @pl.when(k < used)
            def _():
                slot, block = pl.ds(o * slots + k, 1), pl.ds(listed[k], 1)
                copy(mrow.at[slot], nm_ref.at[block], row_sem.at[0]).start()
                copy(wrow.at[slot], nw_ref.at[block], row_sem.at[1]).start(priority=1)

        return issued + used

    issued = lax.fori_loop(0, half, patch, jnp.int32(0))
    for c in later:
        c.wait()
    issued = lax.fori_loop(half, owners, patch, issued)
    size = slots * owners
    while size:
        part = pl.ds(0, size)

        @pl.when((issued & size) != 0)
        def _():
            copy(mrow.at[part], nm_ref.at[part], row_sem.at[0]).wait()
            copy(wrow.at[part], nw_ref.at[part], row_sem.at[1]).wait()

        size //= 2


def local(gradient, residual, weights, momentum, sel_idx, sel_count, gath_idx, gath_count):
    grad, res = gradient[0], residual[0]
    blocks, width = grad.shape
    owners, cap = sel_idx.shape[1:]
    slots = gath_idx.shape[1]
    sel = jnp.transpose(sel_idx, (0, 2, 1)).reshape(owners * cap, owners)
    gath = jnp.transpose(gath_idx, (1, 0))
    full = jax.ShapeDtypeStruct((blocks, width), F32)
    listed_rows = jax.ShapeDtypeStruct((owners * slots, width), F32)
    params = pltpu.CompilerParams(vmem_limit_bytes=VMEM_ALL)

    rows = pl.pallas_call(
        front,
        out_shape=jax.ShapeDtypeStruct((owners * cap, width), F32),
        in_specs=[HBM, HBM, HBM],
        out_specs=VMEM,
        scratch_shapes=[
            pltpu.SMEM((cap, owners), I32),
            pltpu.VMEM((2, owners * cap, width), F32),
            DMA(()),
            DMA((2,)),
        ],
        compiler_params=params,
        cost_estimate=cost(owners * cap * width * 12),
        name="front",
    )(sel, grad, res)
    got = lax.all_to_all(rows.reshape(owners, cap, width), "dp", 0, 0, tiled=True)

    new_residual, hot, plan = pl.pallas_call(
        lambda *refs: middle(cap, *refs),
        out_shape=(full, jax.ShapeDtypeStruct((cap * slots, owners), F32), jax.ShapeDtypeStruct((24, owners), I32)),
        in_specs=[HBM] * 6,
        out_specs=(HBM, HBM, HBM),
        scratch_shapes=[
            pltpu.VMEM((owners * cap, owners), I32),
            pltpu.VMEM((owners, owners), I32),
            pltpu.VMEM((slots, owners), I32),
            pltpu.VMEM((1, owners), I32),
            pltpu.VMEM((cap * slots, owners), F32),
            pltpu.VMEM((24, owners), I32),
            pltpu.SMEM((24, owners), I32),
            pltpu.VMEM((blocks + 8, width), F32),
            pltpu.VMEM((blocks, width), F32),
            DMA((4,)),
            DMA((2, CHUNKS)),
            DMA((CHUNKS,)),
        ],
        compiler_params=pltpu.CompilerParams(vmem_limit_bytes=60_000_000),
        cost_estimate=cost(blocks * width * 12),
        name="middle",
    )(sel, sel_count, gath, gath_count.reshape(1, owners), grad, res)

    shared = pl.pallas_call(
        reduce_rows,
        out_shape=listed_rows,
        in_specs=[VMEM, VMEM],
        out_specs=VMEM,
        compiler_params=pltpu.CompilerParams(vmem_limit_bytes=8 << 20),
        cost_estimate=cost(owners * slots * width * 8),
        name="reduce_rows",
    )(hot, got.reshape(owners * cap, width))
    sums = lax.all_to_all(shared.reshape(owners, slots, width), "dp", 0, 0, tiled=True)

    nw, nm, wrow, mrow = pl.pallas_call(
        early,
        out_shape=(full, full, listed_rows, listed_rows),
        in_specs=[HBM] * 4,
        out_specs=(HBM,) * 4,
        scratch_shapes=[
            pltpu.SMEM((slots, owners), I32),
            pltpu.SMEM((24, owners), I32),
            pltpu.VMEM((owners * slots, width), F32),
            pltpu.VMEM((owners * slots, width), F32),
            pltpu.VMEM((blocks, width), F32),
            pltpu.VMEM((blocks, width), F32),
            DMA((2,)),
            DMA((2, CHUNKS)),
            DMA((2, CHUNKS)),
        ],
        compiler_params=params,
        cost_estimate=cost(blocks * width * 16),
        name="early",
    )(gath, plan, weights, momentum)

    new_weights, new_momentum = pl.pallas_call(
        late,
        out_shape=(full, full),
        in_specs=[HBM] * 7,
        out_specs=(HBM, HBM),
        scratch_shapes=[
            pltpu.SMEM((slots, owners), I32),
            pltpu.SMEM((1, owners), I32),
            pltpu.VMEM((owners * slots, width), F32),
            pltpu.VMEM((owners * slots, width), F32),
            pltpu.VMEM((owners * slots, width), F32),
            DMA((2, 5)),
            DMA((2,)),
        ],
        input_output_aliases={5: 0, 6: 1},
        compiler_params=params,
        cost_estimate=cost(owners * slots * width * 20),
        name="late",
    )(gath, gath_count.reshape(1, owners), sums.reshape(owners * slots, width), wrow, mrow, nw, nm)
    return new_weights, new_momentum, new_residual[None]


def solution(mesh):
    placed = (P("dp", None, None), P("dp", None, None), P(), P(), P(), P(), P(), P())
    return jax.shard_map(
        local,
        mesh=mesh,
        in_specs=placed,
        out_specs=(P(), P(), P("dp", None, None)),
        check_vma=False,
    )
```
